256 devices in a mesh: wide: 64 (over z, y, core), narrow: 4 (over x).
Axes of the slice: x: 4, y: 4, z: 8, core: 2. Of those that a mesh axis runs over, the one named last changes fastest.
Arguments:
- stored_amps: float32 [1024, 16384], P('wide', 'narrow'), may hold values from -6 to 6
- integrals: float32 [16384, 16384], P('narrow', 'wide'), may hold values from -0.046875 to 0.046875
- pair_counts: int32 [4], replicated, may hold values from 2048 to 4096, as said below
- block_map: int32 [64], replicated, may hold values from 0 to 63, each once
Outputs:
- cycle_out: float32 [1024, 16384], P('wide', 'narrow')
The draws below stay inside these ranges and needn't reach their ends.
Inputs may be any that keep to these rules, and one draw needn't show every extreme that they name: `pair_counts`: each count lies between half of 4096 and 4096; one count equals 4096. `block_map`: a permutation of the indices of wide.
All inputs are finite; a program needn't handle non-finite values.
Results may differ from the reference program's by a relative error of at most 0.000086.
Values sent between devices are 32-bit elements; how exact they have to be, the bound alone decides.
No kernel may reach another device: no remote copies, remote signals or barrier semaphores. Data moves between devices by JAX's collectives and lax.ppermute only.
A program may use at most 64 MiB of HBM per device.

```python
import jax
import jax.numpy as jnp
from jax import lax

PB = 4096
Q = 16384
BR = 8
NL = 2
R = 1024
P_SIZE = 16384
G = 64
N_WIDE = 64
N_NARROW = 4


def draw_pair_counts(key, part):
    first, second = jax.random.split(jax.random.fold_in(key, 11))
    values = jax.random.randint(first, (4,), PB // 2, PB + 1)
    chosen = jax.random.randint(second, (), 0, 4)
    return jnp.where(jnp.arange(4) == chosen, PB, values).astype(jnp.int32)


def steps_of(stream_key, dims, cuts, smallest, largest):
    loudness = 1.0
    for position, parts in cuts:
        heights = jax.random.uniform(jax.random.fold_in(jax.random.fold_in(stream_key, 6), position), (parts,), jnp.float32, smallest / len(cuts), largest / len(cuts))
        loudness = loudness * jnp.repeat(jnp.exp(heights), dims[position] // parts).reshape((-1,) + (1,) * (len(dims) - 1 - position))
    return loudness


def scatter_about(rng, shape, scale, reach, pieces=(), held_as=jnp.bfloat16):
    drawn = scale * jax.random.normal(rng, shape, jnp.float32)
    if pieces:
        drawn = drawn * steps_of(rng, shape, pieces, -0.22, 0.18)
    return jnp.clip(drawn, -reach, reach).astype(held_as)


def setup_inputs(seed: int = 0) -> dict:
    keys = jax.random.split(jax.random.key(seed), 5)
    stored_amps = scatter_about(keys[0], (R, P_SIZE), 1.0, 6.0, ((0, 64), (1, 4)), jnp.float32)
    integrals = scatter_about(keys[1], (P_SIZE, Q), P_SIZE ** -0.5, 0.046875, ((0, 4), (1, 64)), jnp.float32)
    pair_counts = draw_pair_counts(jax.random.fold_in(keys[4], 71), 0)
    block_map = jax.random.permutation(keys[3], N_WIDE).astype(jnp.int32)
    return {"stored_amps": stored_amps, "integrals": integrals, "pair_counts": pair_counts, "block_map": block_map}


def reference(stored_amps, integrals, pair_counts, block_map):
    blocks = stored_amps.reshape(N_WIDE, NL, BR, P_SIZE)
    blocks = jnp.take(blocks, block_map, axis=0)
    tamp = jnp.transpose(blocks, (1, 0, 2, 3)).reshape(R, P_SIZE)
    columns = jnp.arange(P_SIZE, dtype=jnp.int32)
    limit = jnp.take(pair_counts, columns // PB)
    tamp = jnp.where((columns % PB < limit)[None, :], tamp, jnp.float32(0.0))
    cycle = jnp.dot(tamp, integrals, precision=lax.Precision.HIGHEST, preferred_element_type=jnp.float32)
    grouped = cycle.reshape(R, N_WIDE, N_NARROW, G)
    return jnp.transpose(grouped, (0, 2, 1, 3)).reshape(R, Q)
```

```python
import jax
import jax.numpy as jnp
import numpy as np
from jax import lax
from jax.sharding import Mesh
from jax.sharding import PartitionSpec as P

PB = 4096
BR = 8


def on_device(stored_amps, integrals, pair_counts, block_map):
    core = lax.axis_index("core")
    layer = lax.axis_index("x")
    nx = lax.axis_size("x")
    width = stored_amps.shape[1]
    rows = stored_amps.shape[0]
    chips = lax.axis_size("z") * lax.axis_size("y")
    depth, cols = integrals.shape
    group = cols // nx
    limit = lax.dynamic_index_in_dim(pair_counts, layer * width // PB, keepdims=False)
    column = lax.broadcasted_iota(jnp.int32, (rows, width), 1)
    masked = jnp.where(column < limit, stored_amps, jnp.float32(0.0))
    gathered = lax.all_gather(masked, ("z", "y"), axis=0, tiled=True)
    swap = [(0, 1), (1, 0)]
    other = lax.ppermute(integrals, "core", swap)
    mine = integrals.reshape(depth, nx, group)
    other = other.reshape(depth, nx, group)
    pair = jnp.concatenate(
        [jnp.where(core == 0, mine, other), jnp.where(core == 0, other, mine)], axis=2
    )
    pair = pair.reshape(depth, nx * 2 * group)
    both = jnp.dot(
        gathered, pair, precision=lax.Precision.HIGH, preferred_element_type=jnp.float32
    )
    total = lax.dynamic_slice_in_dim(both, layer * 2 * group, 2 * group, axis=1)
    for step in (1, 3, 2):
        to = (layer + step) % nx
        part = lax.dynamic_slice_in_dim(both, to * 2 * group, 2 * group, axis=1)
        total = total + lax.ppermute(part, "x", [(i, (i + step) % nx) for i in range(nx)])
    partner = lax.ppermute(total, "core", swap)
    blocks = jnp.concatenate([total, partner], axis=0).reshape(-1, BR, 2 * group)
    target = 2 * jnp.arange(chips, dtype=jnp.int32) + core
    slot = target // chips
    first = 2 * (target % chips)
    owner = jnp.take(block_map, jnp.stack([first, first + 1], axis=1).reshape(-1), axis=0)
    where_is = jnp.where(owner % 2 != core, chips, 0) + owner // 2
    index = where_is * 2 + jnp.repeat(slot, 2)
    chosen = jnp.take(blocks, index, axis=0).reshape(chips, rows, 2 * group)
    moved = lax.all_to_all(chosen, ("z", "y"), split_axis=0, concat_axis=0, tiled=True)
    return jnp.transpose(moved, (1, 0, 2)).reshape(rows, chips * 2 * group)


def solution(mesh):
    fine = Mesh(np.asarray(mesh.devices).reshape(8, 4, 2, 4), ("z", "y", "core", "x"))
    wide = ("z", "y", "core")
    placed = (P(wide, "x"), P("x", wide), P(), P())
    return jax.shard_map(
        on_device, mesh=fine, in_specs=placed, out_specs=P(wide, "x"), check_vma=False
    )
```
